32 devices in a mesh: half: 4 (over y, core), blk: 8 (over z, x).
Axes of the slice: x: 2, y: 2, z: 4, core: 2. Of those that a mesh axis runs over, the one named last changes fastest.
Arguments:
- sketch: float32 [32768, 256], P(('half', 'blk')), may hold values from -6 to 6
- near_field: float32 [32768, 256], P(('half', 'blk')), may hold values from -0.375 to 0.375
- source_one: float32 [32768, 128], P(('half', 'blk')), may hold values from -0.5 to 0.5
- source_two: float32 [32768, 128], P(('half', 'blk')), may hold values from -0.5 to 0.5
- target_one: float32 [32768, 128], P(('half', 'blk')), may hold values from -0.5 to 0.5
- target_two: float32 [32768, 128], P(('half', 'blk')), may hold values from -0.5 to 0.5
- quarter_mix: float32 [256, 2, 128, 128], P(('half', 'blk')), may hold values from -0.375 to 0.375
- leaf_mix: float32 [256, 2, 128, 128], P(('half', 'blk')), may hold values from -0.375 to 0.375
- target_mix_one: float32 [256, 2, 128, 128], P(('half', 'blk')), may hold values from -0.375 to 0.375
- target_mix_two: float32 [256, 2, 128, 128], P(('half', 'blk')), may hold values from -0.375 to 0.375
Outputs:
- product: float32 [32768, 256], P(('half', 'blk'))
The draws below stay inside these ranges and needn't reach their ends.
All inputs are finite; a program needn't handle non-finite values.
Results may differ from the reference program's by a relative error of at most 0.000061.
Values sent between devices are 32-bit elements; how exact they have to be, the bound alone decides.
No kernel may reach another device: no remote copies, remote signals or barrier semaphores. Data moves between devices by JAX's collectives and lax.ppermute only.
A program may use at most 128 MiB of HBM per device.

```python
import jax
import jax.numpy as jnp
from jax import lax

RANK = 128
VECS = 256
GROUP = 8
LEAF = 128
ROWS = 32768
NODES = 256


def block_scale(stream_key, extent, shards, least, largest):
    gain = 1.0
    for axis_at, parts in shards:
        steps = jax.random.uniform(jax.random.fold_in(jax.random.fold_in(stream_key, 6), axis_at), (parts,), jnp.float32, least / len(shards), largest / len(shards))
        gain = gain * jnp.repeat(jnp.exp(steps), extent[axis_at] // parts).reshape((-1,) + (1,) * (len(extent) - 1 - axis_at))
    return gain


def normal_values(key, dims, width, limit, shards=(), kind=jnp.bfloat16):
    drawn = width * jax.random.normal(key, dims, jnp.float32)
    if shards:
        drawn = drawn * block_scale(key, dims, shards, -0.22, 0.18)
    return jnp.clip(drawn, -limit, limit).astype(kind)


def setup_inputs(seed: int = 0) -> dict:
    key_of = jax.random.split(jax.random.key(seed), 11)
    sketch = normal_values(key_of[0], (ROWS, VECS), 1.0, 6.0, ((0, 32),), jnp.float32)
    near_field = normal_values(key_of[1], (ROWS, 2 * LEAF), (2 * LEAF) ** -0.5, 0.375, ((0, 32),), jnp.float32)
    source_one = normal_values(key_of[2], (ROWS, RANK), LEAF ** -0.5, 0.5, ((0, 32),), jnp.float32)
    source_two = normal_values(key_of[3], (ROWS, RANK), LEAF ** -0.5, 0.5, ((0, 32),), jnp.float32)
    target_one = normal_values(key_of[4], (ROWS, RANK), RANK ** -0.5, 0.5, ((0, 32),), jnp.float32)
    target_two = normal_values(key_of[5], (ROWS, RANK), RANK ** -0.5, 0.5, ((0, 32),), jnp.float32)
    quarter_mix = normal_values(key_of[6], (NODES, 2, RANK, RANK), (2 * RANK) ** -0.5, 0.375, ((0, 32),), jnp.float32)
    leaf_mix = normal_values(key_of[7], (NODES, 2, RANK, RANK), (2 * RANK) ** -0.5, 0.375, ((0, 32),), jnp.float32)
    target_mix_one = normal_values(key_of[8], (NODES, 2, RANK, RANK), (2 * RANK) ** -0.5, 0.375, ((0, 32),), jnp.float32)
    target_mix_two = normal_values(key_of[9], (NODES, 2, RANK, RANK), (2 * RANK) ** -0.5, 0.375, ((0, 32),), jnp.float32)
    return dict(sketch=sketch, near_field=near_field, source_one=source_one, source_two=source_two, target_one=target_one, target_two=target_two, quarter_mix=quarter_mix, leaf_mix=leaf_mix, target_mix_one=target_mix_one, target_mix_two=target_mix_two)


highest = lax.Precision.HIGHEST


def leaf_view(array, columns):
    return array.reshape(4, GROUP, GROUP, LEAF, columns)


def node_view(matrices, member):
    return matrices.reshape(4, GROUP, GROUP, 2, RANK, RANK)[:, :, :, member]


def apply_nodes(matrices, coefficients):
    return jnp.einsum('qbkst,qbktv->qbksv', matrices, coefficients, precision=highest)


def apply_back(matrices, coefficients):
    return jnp.einsum('qbkts,qbktv->qbksv', matrices, coefficients, precision=highest)


def flip_quarter(coefficients, level_bit):
    shaped = coefficients.reshape((2, 2) + coefficients.shape[1:])
    if level_bit == 1:
        shaped = shaped[::-1]
    else:
        shaped = shaped[:, ::-1]
    return shaped.reshape(coefficients.shape)


def flip_leaf(coefficients):
    shaped = coefficients.reshape(4, GROUP, GROUP // 2, 2, RANK, VECS)
    return shaped[:, :, :, ::-1].reshape(coefficients.shape)


def transport(coefficients, level_bit):
    return flip_quarter(coefficients, level_bit).transpose(0, 2, 1, 3, 4)


def compress(basis, operand):
    return jnp.einsum('qblir,qbliv->qblrv', leaf_view(basis, RANK), leaf_view(operand, VECS), precision=highest)


def expand(basis, coefficients):
    result = jnp.einsum('qblir,qblrv->qbliv', leaf_view(basis, RANK), coefficients, precision=highest)
    return result.reshape(ROWS, VECS)


def near_apply(near_field, operand, pattern):
    near_boxes = near_field.reshape(4, GROUP, GROUP // 2, 2 * LEAF, 2 * LEAF)
    blocks = operand.reshape(4, GROUP, GROUP // 2, 2 * LEAF, VECS)
    return jnp.einsum(pattern, near_boxes, blocks, precision=highest).reshape(ROWS, VECS)


def reference(sketch, near_field, source_one, source_two, target_one, target_two, quarter_mix, leaf_mix, target_mix_one, target_mix_two):
    coef_one = compress(source_one, sketch)
    mixed_one = apply_nodes(node_view(quarter_mix, 0), coef_one) + apply_nodes(node_view(quarter_mix, 1), flip_quarter(coef_one, 0))
    arrived_one = transport(mixed_one, 1)
    out_one = apply_nodes(node_view(target_mix_one, 0), arrived_one) + apply_nodes(node_view(target_mix_one, 1), flip_leaf(arrived_one))
    coef_two = compress(source_two, sketch)
    mixed_two = apply_nodes(node_view(leaf_mix, 0), coef_two) + apply_nodes(node_view(leaf_mix, 1), flip_leaf(coef_two))
    arrived_two = transport(mixed_two, 0)
    out_two = apply_nodes(node_view(target_mix_two, 0), arrived_two) + apply_nodes(node_view(target_mix_two, 1), flip_leaf(arrived_two))
    sketched = 0.5 * sketch + near_apply(near_field, sketch, 'qbkij,qbkjv->qbkiv') + expand(target_one, out_one) + expand(target_two, out_two)

    head_one = compress(target_one, sketched)
    back_one = apply_back(node_view(target_mix_one, 0), head_one) + flip_leaf(apply_back(node_view(target_mix_one, 1), head_one))
    landed_one = transport(back_one, 1)
    tail_one = apply_back(node_view(quarter_mix, 0), landed_one) + flip_quarter(apply_back(node_view(quarter_mix, 1), landed_one), 0)
    head_two = compress(target_two, sketched)
    back_two = apply_back(node_view(target_mix_two, 0), head_two) + flip_leaf(apply_back(node_view(target_mix_two, 1), head_two))
    landed_two = transport(back_two, 0)
    tail_two = apply_back(node_view(leaf_mix, 0), landed_two) + flip_leaf(apply_back(node_view(leaf_mix, 1), landed_two))
    product = 0.5 * sketched + near_apply(near_field, sketched, 'qbkji,qbkjv->qbkiv') + expand(source_one, tail_one) + expand(source_two, tail_two)
    return product
```

```python
import functools

import jax
import jax.numpy as jnp
from jax import lax
from jax.experimental import pallas as pl
from jax.experimental.pallas import tpu as pltpu
from jax.sharding import PartitionSpec as P


ANY = pl.BlockSpec(memory_space=pl.ANY)
VMEM = pl.BlockSpec(memory_space=pltpu.VMEM)


def send(block, turn, flip):
    halves, blks = lax.axis_size("half"), lax.axis_size("blk")
    route = [
        (q * blks + b, (q ^ turn) * blks + (b ^ flip)) for q in range(halves) for b in range(blks)
    ]
    return lax.ppermute(block, ("half", "blk"), route)


def place(r):
    spot = lax.axis_index("blk")
    parity = jnp.bitwise_and(spot, 1)
    return jnp.bitwise_xor(lax.div(spot, 2), r), (parity, 1 - parity)


def split(x):
    top = x.astype(jnp.bfloat16)
    return top, (x - top.astype(jnp.float32)).astype(jnp.bfloat16)


def dot(left, right, left_axis=1):
    def one(a, b):
        return lax.dot_general(
            a, b, (((left_axis,), (0,)), ((), ())), preferred_element_type=jnp.float32
        )

    (a, a_low), (b, b_low) = split(left), split(right)
    return one(a, b) + (one(a, b_low) + one(a_low, b))


def side(matrix, axis=0):
    return jnp.concatenate(matrix, axis=axis)


def copies(sources, targets, sems):
    started = []
    for at, (source, target) in enumerate(zip(sources, targets)):
        started.append(pltpu.make_async_copy(source, target, sems.at[at]))
        started[-1].start()
    return started


def wait(started):
    for copy in started:
        copy.wait()


def box(ref, k, size):
    return ref.at[pl.ds(k * size, size)]


def call(kernel, outs, scratch, count, in_specs, out_specs=None, **options):
    return pl.pallas_call(
        kernel,
        out_shape=outs,
        in_specs=in_specs,
        out_specs=out_specs if out_specs is not None else [VMEM] * len(outs),
        scratch_shapes=list(scratch) + [pltpu.SemaphoreType.DMA((count,))],
        compiler_params=pltpu.CompilerParams(vmem_limit_bytes=12 << 20),
        **options,
    )


def rows_of(ref, at, leaf):
    return ref[pl.ds(at * leaf, leaf), :]


def f32(*shape):
    return jax.ShapeDtypeStruct(shape, jnp.float32)


def buf(*shape):
    return pltpu.VMEM(shape, jnp.float32)


def quarter_source(r, leaf, sketch, source, mix, out_0, out_1, v, s, m, sems):
    k, sides = place(r)
    started = copies(
        (box(sketch, k, 2 * leaf), box(source, k, 2 * leaf), box(mix, k, 2)), (v, s, m), sems
    )
    wait(started[:2])
    coef = side([dot(rows_of(s, at, leaf), rows_of(v, at, leaf), 0) for at in range(2)])
    wait(started[2:])
    for out, at in zip((out_0, out_1), sides):
        straight, cross = m[at, 0], m[at, 1]
        first = jnp.where(at == 0, straight, cross)
        second = jnp.where(at == 0, cross, straight)
        out[...] = dot(side([first, second], 1), coef)


def half_source(leaf, leaves, sketch, source, out):
    for at in range(leaves):
        out[at] = dot(rows_of(source, at, leaf), rows_of(sketch, at, leaf), 0)


def half_mix(r, coef, other, mix, out_0, out_1, c, o, m, sems):
    k, sides = place(r)
    wait(copies((box(coef, k, 2), box(other, k, 2), box(mix, k, 2)), (c, o, m), sems))
    for out, at in zip((out_0, out_1), sides):
        out[...] = dot(side([m[at, 0], m[at, 1]], 1), side([c[at], o[at]]))


def turn_round(
    r, leaf, sketch, near, base_1, base_2, mix_1, mix_2, in_10, in_11, in_20, in_21,
    middle, out_10, out_11, out_20, out_21, v, n, b_1, b_2, m_1, m_2, sems,
):
    k, sides = place(r)
    rows = 2 * leaf
    started = copies(
        (
            box(mix_1, k, 2),
            box(mix_2, k, 2),
            box(sketch, k, rows),
            box(near, k, rows),
            box(base_1, k, rows),
            box(base_2, k, rows),
        ),
        (m_1, m_2, v, n, b_1, b_2),
        sems,
    )
    wait(started)
    mixes = []
    gains = []
    for m, ins in ((m_1, (in_10, in_11)), (m_2, (in_20, in_21))):
        mixer = side(
            [
                side([m[sides[0], 0], m[sides[0], 1]], 1),
                side([m[sides[1], 1], m[sides[1], 0]], 1),
            ]
        )
        mixes.append(mixer)
        gains.append(dot(mixer, side([ins[0][...], ins[1][...]])))
    rank = gains[0].shape[0] // 2
    heads = []
    for j, at in enumerate(sides):
        basis = side([rows_of(b_1, at, leaf), rows_of(b_2, at, leaf)], 1)
        gain = side([g[j * rank : (j + 1) * rank] for g in gains])
        total = (
            0.5 * rows_of(v, at, leaf)
            + dot(rows_of(n, at, leaf), v[...])
            + dot(basis, gain)
        )
        middle[pl.ds(at * leaf, leaf), :] = total
        heads.append(dot(basis, total, 0))
    for level, (mixer, outs) in enumerate(zip(mixes, ((out_10, out_11), (out_20, out_21)))):
        head = side([h[level * rank : (level + 1) * rank] for h in heads])
        back = dot(mixer, head, 0)
        outs[0][...] = back[:rank]
        outs[1][...] = back[rank:]


def half_back(r, in_0, in_1, mix, kept, sent, m, sems):
    k, sides = place(r)
    wait(copies((box(mix, k, 2),), (m,), sems))
    for j, (landed, at) in enumerate(zip((in_0, in_1), sides)):
        rank = landed.shape[0]
        both = dot(side([m[at, 0], m[at, 1]], 1), landed[...], 0)
        kept[j] = both[:rank]
        sent[j] = both[rank:]


def finish(
    r, leaf, chained, near, base_1, base_2, mix, middle, kept, other, in_0, in_1, *rest
):
    out, n, b_1, b_2, m, result, sems, out_sem = rest[1:] if chained else rest
    k, sides = place(r)
    rows = 2 * leaf
    wait(
        copies(
            (box(near, k, rows), box(base_1, k, rows), box(base_2, k, rows), box(mix, k, 2)),
            (n, b_1, b_2, m),
            sems,
        )
    )
    mixer = side(
        [side([m[sides[0], 0], m[sides[0], 1]], 1), side([m[sides[1], 1], m[sides[1], 0]], 1)]
    )
    rank = in_0.shape[0]
    tail = dot(mixer, side([in_0[...], in_1[...]]), 0)
    result[...] = 0.5 * middle[...] + dot(n[...], middle[...], 0)
    for j, at in enumerate(sides):
        basis = side([rows_of(b_1, at, leaf), rows_of(b_2, at, leaf)], 1)
        both = side([kept[j] + other[j], tail[j * rank : (j + 1) * rank]])
        result[pl.ds(at * leaf, leaf), :] += dot(basis, both)
    store = pltpu.make_async_copy(result, box(out, k, rows), out_sem)
    store.start()
    store.wait()


def body(
    sketch,
    near_field,
    source_one,
    source_two,
    target_one,
    target_two,
    quarter_mix,
    leaf_mix,
    target_mix_one,
    target_mix_two,
):
    leaves = lax.axis_size("blk")
    leaf = sketch.shape[0] // leaves
    rows, vecs, rank = 2 * leaf, sketch.shape[1], source_one.shape[1]
    order = []
    span = leaves // 2
    while span > 1:
        order += range(span // 2, span)
        span //= 2
    order.append(0)
    node, mixer, basis = f32(rank, vecs), buf(2, 2, rank, rank), buf(rows, rank)
    pair = f32(2, rank, vecs)

    def fetch_two(r):
        return call(
            functools.partial(quarter_source, r, leaf), [node] * 2, [buf(rows, vecs), basis, mixer],
            3, [ANY] * 3, name=f"quarter_source_{r}",
        )(sketch, source_two, leaf_mix)

    def fetch_one(r, coef, other):
        return call(
            functools.partial(half_mix, r), [node] * 2,
            [buf(2, rank, vecs), buf(2, rank, vecs), mixer], 3, [ANY] * 3, name=f"half_mix_{r}",
        )(coef, other, quarter_mix)

    forward = {}
    first = order[0]
    forward[first] = [send(x, 1, 2 * first + j) for j, x in enumerate(fetch_two(first))]
    coef = pl.pallas_call(
        functools.partial(half_source, leaf, leaves), out_shape=f32(leaves, rank, vecs),
        in_specs=[VMEM] * 2, out_specs=VMEM, name="half_source",
        compiler_params=pltpu.CompilerParams(vmem_limit_bytes=12 << 20),
    )(sketch, source_one)
    other = send(coef, 1, 0)
    for r in order:
        if r != first:
            forward[r] = [send(x, 1, 2 * r + j) for j, x in enumerate(fetch_two(r))]
        ones = [send(x, 2, 2 * r + j) for j, x in enumerate(fetch_one(r, coef, other))]
        forward[r] = ones + forward[r]

    backward, middles = {}, {}
    for r in order:
        middles[r], *outs = call(
            functools.partial(turn_round, r, leaf), [f32(rows, vecs)] + [node] * 4,
            [buf(rows, vecs), buf(rows, near_field.shape[1]), basis, basis, mixer, mixer],
            6, [ANY] * 6 + [VMEM] * 4, name=f"turn_round_{r}",
        )(
            sketch, near_field, target_one, target_two, target_mix_one, target_mix_two,
            *forward[r],
        )
        backward[r] = [
            send(x, 2 - j // 2, 2 * r + j % 2) for j, x in enumerate(outs)
        ]

    product = None
    for r in reversed(order) if False else order:
        one, two = backward[r][:2], backward[r][2:]
        kept, sent = call(
            functools.partial(half_back, r), [pair] * 2, [mixer], 1, [VMEM] * 2 + [ANY],
            name=f"half_back_{r}",
        )(*one, quarter_mix)
        chained = product is not None
        operands = [
            near_field, source_one, source_two, leaf_mix, middles[r], kept, send(sent, 1, 0), *two,
        ]
        specs = [ANY] * 4 + [VMEM] * 5
        options = {}
        if chained:
            options["input_output_aliases"] = {len(operands): 0}
            operands.append(product)
            specs.append(ANY)
        (product,) = pl.pallas_call(
            functools.partial(finish, r, leaf, chained),
            out_shape=[f32(*sketch.shape)],
            in_specs=specs,
            out_specs=[ANY],
            scratch_shapes=[
                buf(rows, near_field.shape[1]), basis, basis, mixer, buf(rows, vecs),
                pltpu.SemaphoreType.DMA((4,)), pltpu.SemaphoreType.DMA(()),
            ],
            compiler_params=pltpu.CompilerParams(vmem_limit_bytes=12 << 20),
            name=f"finish_{r}",
            **options,
        )(*operands)
    return product


def solution(mesh):
    flat = P(("half", "blk"), None)
    deep = P(("half", "blk"), None, None, None)
    return jax.shard_map(
        body, mesh=mesh, in_specs=(flat,) * 6 + (deep,) * 4, out_specs=flat, check_vma=False
    )
```
